32 devices in a mesh: tm: 8 (over y, x, core), batch: 4 (over z).
Axes of the slice: x: 2, y: 2, z: 4, core: 2. Of those that a mesh axis runs over, the one named last changes fastest.
Arguments:
- hidden_states: bfloat16 [4, 1024, 5120], P('batch', 'tm'), may hold values from -6 to 6
- gen_weight: bfloat16 [64, 5120], replicated, may hold values from -0.078125 to 0.078125
- noise_field: bfloat16 [4, 64, 1024], P('batch', None, 'tm'), may hold values from -6 to 6
- timesteps: int32 [4], P('batch'), may hold values from 200 to 999
- embed_real: bfloat16 [128, 5120], replicated, may hold values from -0.5 to 0.5
- time_real: bfloat16 [256, 3, 5120], P('tm'), may hold values from -0.375 to 0.375
- query_real: bfloat16 [5120, 1024], P(None, 'tm'), may hold values from -3 to 3
- key_real: bfloat16 [5120, 1024], P(None, 'tm'), may hold values from -3 to 3
- value_real: bfloat16 [5120, 1024], P(None, 'tm'), may hold values from -0.078125 to 0.078125
- out_real: bfloat16 [1024, 5120], P('tm'), may hold values from -0.1875 to 0.1875
- gain_real: float32 [2, 1024], P(None, 'tm'), may hold values from 0.25 to 3
- proj_real: bfloat16 [64, 5120], replicated, may hold values from -0.078125 to 0.078125
- embed_fake: bfloat16 [128, 5120], replicated, may hold values from -0.5 to 0.5
- time_fake: bfloat16 [256, 3, 5120], P('tm'), may hold values from -0.375 to 0.375
- query_fake: bfloat16 [5120, 1024], P(None, 'tm'), may hold values from -3 to 3
- key_fake: bfloat16 [5120, 1024], P(None, 'tm'), may hold values from -3 to 3
- value_fake: bfloat16 [5120, 1024], P(None, 'tm'), may hold values from -0.078125 to 0.078125
- out_fake: bfloat16 [1024, 5120], P('tm'), may hold values from -0.1875 to 0.1875
- gain_fake: float32 [2, 1024], P(None, 'tm'), may hold values from 0.25 to 3
- proj_fake: bfloat16 [64, 5120], replicated, may hold values from -0.078125 to 0.078125
Outputs:
- dmd_gradient: float32 [4, 64, 1024], P('batch', None, 'tm')
- weight_grad: float32 [64, 5120], replicated
The draws below stay inside these ranges and needn't reach their ends.
All inputs are finite; a program needn't handle non-finite values.
Results may differ from the reference program's by a relative error of at most 0.019.
Values may be sent and summed in bfloat16 or wider, within the bound.
No kernel may reach another device: no remote copies, remote signals or barrier semaphores. Data moves between devices by JAX's collectives and lax.ppermute only.
A program may use at most 128 MiB of HBM per device.

```python
import math
import jax
import jax.numpy as jnp
from jax import lax

D = 5120
HD = 128
FREQ = 256
FTOK = 128
HEADS = 8
PATCH = 64
KIN = 128
TOKENS = 1024
SAMPLES = 4


def spiked_pair(key, salt_value):
    base_key = jax.random.fold_in(key, salt_value)
    key_one, key_two, key_three, key_four = jax.random.split(base_key, 4)
    proj_width = HEADS * HD
    query_draw = jax.random.normal(key_one, (D, proj_width), jnp.float32) / math.sqrt(D)
    key_draw = jax.random.normal(key_four, (D, proj_width), jnp.float32) / math.sqrt(D)
    return (jnp.clip(query_draw, -3.0, 3.0), jnp.clip(key_draw, -3.0, 3.0))


def draw_query_real(key, part):
    return spiked_pair(key, 11)[0].astype(jnp.bfloat16)


def draw_key_real(key, part):
    return spiked_pair(key, 11)[1].astype(jnp.bfloat16)


def draw_query_fake(key, part):
    return spiked_pair(key, 23)[0].astype(jnp.bfloat16)


def draw_key_fake(key, part):
    return spiked_pair(key, 23)[1].astype(jnp.bfloat16)


def touch_ends(drawn, key, smallest, largest):
    longest = drawn.shape.index(max(drawn.shape))
    spots = []
    for shift in (0, 1):
        where = [jax.random.randint(jax.random.fold_in(key, axis), (), 0, length) for axis, length in enumerate(drawn.shape)]
        where[longest] = (where[longest] + shift) % drawn.shape[longest]
        spots.append(tuple(where))
    return drawn.at[spots[0]].set(smallest).at[spots[1]].set(largest)


def level_of(key, extent, shards, low, top_value):
    def one(position, parts):
        steps = jax.random.uniform(jax.random.fold_in(jax.random.fold_in(key, 6), position), (parts,), jnp.float32, low / len(shards), top_value / len(shards))
        return jnp.repeat(jnp.exp(steps), extent[position] // parts).reshape((-1,) + (1,) * (len(extent) - position - 1))

    factor_of = one(*shards[0])
    for cut in shards[1:]:
        factor_of = factor_of * one(*cut)
    return factor_of


def scatter_about(rng, dims, deviation, most, cuts=(), kind=jnp.bfloat16):
    factor_of = level_of(rng, dims, cuts, -0.22, 0.18) if cuts else 1.0
    values = jax.random.normal(rng, dims, jnp.float32) * deviation * factor_of
    return jnp.minimum(jnp.maximum(values, -most), most).astype(kind)


def setup_inputs(seed: int = 0) -> dict:
    seeds = jax.random.split(jax.random.key(seed), 21)
    hidden_states = scatter_about(seeds[0], (SAMPLES, TOKENS, D), 1.0, 6.0, ((0, 4), (1, 8)))
    gen_weight = scatter_about(seeds[1], (PATCH, D), D ** -0.5, 0.078125)
    noise_field = scatter_about(seeds[2], (SAMPLES, PATCH, TOKENS), 1.0, 6.0, ((0, 4), (2, 8)))
    timesteps = touch_ends(jax.random.randint(seeds[3], (SAMPLES,), 200, 1000), jax.random.fold_in(seeds[3], 1), 200, 999).astype(jnp.int32)
    embed_real = scatter_about(seeds[4], (KIN, D), KIN ** -0.5, 0.5)
    time_real = scatter_about(seeds[5], (FREQ, 3, D), FREQ ** -0.5, 0.375, ((0, 8),))
    query_real = draw_query_real(jax.random.fold_in(seeds[20], 71), 0)
    key_real = draw_key_real(jax.random.fold_in(seeds[20], 71), 0)
    value_real = scatter_about(seeds[8], (D, HEADS * HD), D ** -0.5, 0.078125, ((1, 8),))
    out_real = scatter_about(seeds[9], (HEADS * HD, D), (HEADS * HD) ** -0.5, 0.1875, ((0, 8),))
    gain_real = jnp.clip(jnp.exp(math.log(3.0) - 2.4849066 * jax.random.uniform(seeds[10], (2, HEADS * HD), jnp.float32) ** level_of(seeds[10], (2, HEADS * HD), ((1, 8),), -0.2, 0.2)), 0.25, 3.0)
    proj_real = scatter_about(seeds[11], (PATCH, D), D ** -0.5, 0.078125)
    embed_fake = scatter_about(seeds[12], (KIN, D), KIN ** -0.5, 0.5)
    time_fake = scatter_about(seeds[13], (FREQ, 3, D), FREQ ** -0.5, 0.375, ((0, 8),))
    query_fake = draw_query_fake(jax.random.fold_in(seeds[20], 71), 0)
    key_fake = draw_key_fake(jax.random.fold_in(seeds[20], 71), 0)
    value_fake = scatter_about(seeds[16], (D, HEADS * HD), D ** -0.5, 0.078125, ((1, 8),))
    out_fake = scatter_about(seeds[17], (HEADS * HD, D), (HEADS * HD) ** -0.5, 0.1875, ((0, 8),))
    gain_fake = jnp.clip(jnp.exp(math.log(3.0) - 2.4849066 * jax.random.uniform(seeds[18], (2, HEADS * HD), jnp.float32) ** level_of(seeds[18], (2, HEADS * HD), ((1, 8),), -0.2, 0.2)), 0.25, 3.0)
    proj_fake = scatter_about(seeds[19], (PATCH, D), D ** -0.5, 0.078125)
    return dict(hidden_states=hidden_states, gen_weight=gen_weight, noise_field=noise_field, timesteps=timesteps, embed_real=embed_real, time_real=time_real, query_real=query_real, key_real=key_real, value_real=value_real, out_real=out_real, gain_real=gain_real, proj_real=proj_real, embed_fake=embed_fake, time_fake=time_fake, query_fake=query_fake, key_fake=key_fake, value_fake=value_fake, out_fake=out_fake, gain_fake=gain_fake, proj_fake=proj_fake)


norm_floor = 0.05
gap_floor = 0.25
highest = lax.Precision.HIGHEST

def sinusoid(time_step):
    half_freq = FREQ // 2
    frequency = jnp.exp(-math.log(10000.0) * jnp.arange(half_freq, dtype=jnp.float32) / half_freq)
    angles = time_step.astype(jnp.float32) * frequency
    return jnp.concatenate([jnp.cos(angles), jnp.sin(angles)]).astype(jnp.bfloat16)

def rms_round(vector, gain_row):
    return (vector * lax.rsqrt(lax.optimization_barrier(jnp.mean(vector * vector, axis=1, keepdims=True)) + norm_floor) * gain_row[None, :]).astype(jnp.bfloat16)

def velocity(noisy_patch, sinus_wave, embed_table, time_table, query_proj, key_proj, value_proj, out_proj, norm_gains, final_proj):
    earlier = jnp.concatenate([jnp.zeros((PATCH, FTOK), jnp.bfloat16), noisy_patch[:, :TOKENS - FTOK]], axis=1)
    stacked = jnp.concatenate([noisy_patch, earlier], axis=0)
    embedded = lax.dot_general(stacked, embed_table, (((0,), (0,)), ((), ())), preferred_element_type=jnp.float32)
    row_mean = lax.optimization_barrier(jnp.mean(embedded, axis=1, keepdims=True))
    centered = embedded - row_mean
    rscale = lax.rsqrt(lax.optimization_barrier(jnp.mean(centered * centered, axis=1, keepdims=True)) + norm_floor)
    modulation = jnp.einsum('f,fcd->cd', sinus_wave.astype(jnp.float32), time_table.astype(jnp.float32))
    normed = centered * rscale * (1.0 + modulation[1])[None, :] + modulation[0][None, :]
    queries = jnp.dot(normed, query_proj.astype(jnp.float32), precision=highest)
    keys_all = jnp.dot(normed, key_proj.astype(jnp.float32), precision=highest)
    values_all = jnp.dot(normed, value_proj.astype(jnp.float32), precision=highest).astype(jnp.bfloat16)
    query_norm = rms_round(queries, norm_gains[0])
    key_norm = rms_round(keys_all, norm_gains[1])
    frames = jnp.arange(TOKENS, dtype=jnp.int32) // FTOK
    allowed = frames[None, :] <= frames[:, None]

    def one_head(head_index):
        start_col = head_index * HD
        query_head = lax.dynamic_slice_in_dim(query_norm, start_col, HD, 1)
        key_head = lax.dynamic_slice_in_dim(key_norm, start_col, HD, 1)
        value_head = lax.dynamic_slice_in_dim(values_all, start_col, HD, 1)
        scores = jnp.dot(query_head, key_head.T, preferred_element_type=jnp.float32) / math.sqrt(HD)
        scores = jnp.where(allowed, scores, -1e+30)
        row_peak = lax.optimization_barrier(jnp.max(scores, axis=1, keepdims=True))
        exp_scores = jnp.exp(scores - row_peak)
        attn_probs = (exp_scores / lax.optimization_barrier(jnp.sum(exp_scores, axis=1, keepdims=True))).astype(jnp.bfloat16)
        return jnp.dot(attn_probs, value_head, preferred_element_type=jnp.float32).astype(jnp.bfloat16)
    per_head = lax.map(one_head, jnp.arange(HEADS, dtype=jnp.int32))
    attended = jnp.transpose(per_head, (1, 0, 2)).reshape(TOKENS, HEADS * HD)
    mixed = jnp.dot(attended, out_proj, preferred_element_type=jnp.float32)
    residual = embedded + mixed * modulation[2][None, :]
    return lax.dot_general(final_proj.astype(jnp.float32), residual, (((1,), (1,)), ((), ())), precision=highest)

def reference(hidden_states, gen_weight, noise_field, timesteps, embed_real, time_real, query_real, key_real, value_real, out_real, gain_real, proj_real, embed_fake, time_fake, query_fake, key_fake, value_fake, out_fake, gain_fake, proj_fake):
    grad_root = math.sqrt(SAMPLES * TOKENS)
    gradients = []
    grad_total = jnp.zeros((PATCH, D), jnp.float32)
    for sample in range(SAMPLES):
        time_step = timesteps[sample]
        level_raw = time_step.astype(jnp.float32) / 1000.0
        noise_level = 5.0 * level_raw / (1.0 + 4.0 * level_raw)
        generated = lax.dot_general(gen_weight, hidden_states[sample], (((1,), (1,)), ((), ())), preferred_element_type=jnp.float32).astype(jnp.bfloat16)
        noisy_patch = ((1.0 - noise_level) * generated.astype(jnp.float32) + noise_level * noise_field[sample].astype(jnp.float32)).astype(jnp.bfloat16)
        sinus_wave = sinusoid(time_step)
        vel_real = velocity(noisy_patch, sinus_wave, embed_real, time_real, query_real, key_real, value_real, out_real, gain_real, proj_real)
        vel_fake = velocity(noisy_patch, sinus_wave, embed_fake, time_fake, query_fake, key_fake, value_fake, out_fake, gain_fake, proj_fake)
        pred_real = noisy_patch.astype(jnp.float32) - noise_level * vel_real
        pred_fake = noisy_patch.astype(jnp.float32) - noise_level * vel_fake
        gap_mean = jnp.sum(jnp.abs(generated.astype(jnp.float32) - pred_real)) / (PATCH * TOKENS)
        normalizer = jnp.maximum(gap_mean, gap_floor)
        gap_diff = pred_fake - pred_real
        gradients.append(gap_diff / normalizer)
        difference = gap_diff.astype(jnp.bfloat16)
        partial_grad = jnp.dot(difference, hidden_states[sample], preferred_element_type=jnp.float32)
        grad_total = grad_total + partial_grad / normalizer / grad_root
    return (jnp.stack(gradients), grad_total)
```

```python
import math

import jax
import jax.numpy as jnp
from jax import lax
from jax.sharding import PartitionSpec as P

HD = 128
FREQ = 256
FTOK = 128


norm_floor = 0.05
gap_floor = 0.25


def sinusoid(time_step):
    half_freq = FREQ // 2
    frequency = jnp.exp(-math.log(10000.0) * jnp.arange(half_freq, dtype=jnp.float32) / half_freq)
    angles = time_step.astype(jnp.float32) * frequency
    return jnp.concatenate([jnp.cos(angles), jnp.sin(angles)]).astype(jnp.bfloat16)


def split_two(wide):
    top = lax.reduce_precision(wide, 8, 7)
    return top.astype(jnp.bfloat16), (wide - top).astype(jnp.bfloat16)


def dot32(left, right, left_dim, right_dim):
    return lax.dot_general(
        left, right, (((left_dim,), (right_dim,)), ((), ())), preferred_element_type=jnp.float32
    )


def centre(embed_table):
    wide = embed_table.astype(jnp.float32)
    return wide - jnp.mean(wide, axis=1, keepdims=True)


def gram_of(centered):
    top, low = split_two(centered)
    cross = dot32(top, low, 1, 1)
    return (dot32(top, top, 1, 1) + cross + cross.T) / centered.shape[1]


def fold_heads(centered, shift, scale, weights):
    rows = jnp.concatenate(
        [centered * (1.0 + scale)[None, :], jnp.broadcast_to(shift[None, :], (16, shift.shape[0]))]
    )
    count = rows.shape[0]
    both = jnp.concatenate(split_two(rows))
    folded = [dot32(both, weight, 1, 0) for weight in weights]
    folded = [piece[:count] + piece[count:] for piece in folded]
    kin_rows = centered.shape[0]
    main = jnp.concatenate([piece[:kin_rows] for piece in folded], axis=1)
    offset = jnp.concatenate([piece[kin_rows] for piece in folded])
    return main, offset


def project(token_rows, gram, main, offset):
    kin = token_rows.shape[1]
    table = jnp.concatenate(split_two(jnp.concatenate([main, gram], axis=1)))
    twice = jnp.concatenate([token_rows, token_rows], axis=1)
    product = dot32(twice, table, 1, 0)
    width = main.shape[1]
    variance = jnp.sum(product[:, width:] * token_rows.astype(jnp.float32), axis=1)
    rscale = lax.rsqrt(jnp.maximum(variance, 0.0) + norm_floor)
    return rscale[:, None] * product[:, :width] + offset[None, :]


def rms_round(vector, total_sq, columns, gain_row):
    return (
        vector * lax.rsqrt(total_sq / columns + norm_floor)[:, None] * gain_row[None, :]
    ).astype(jnp.bfloat16)


def attend(query_norm, key_norm, value_norm):
    tokens = query_norm.shape[1]
    block = min(256, tokens)
    frames = jnp.arange(tokens, dtype=jnp.int32) // FTOK
    pieces = []
    for start in range(0, tokens, block):
        stop = start + block
        scores = jnp.einsum(
            "hqd,hkd->hqk",
            query_norm[:, start:stop],
            key_norm[:, :stop],
            preferred_element_type=jnp.float32,
        ) / math.sqrt(HD)
        allowed = frames[None, :stop] <= frames[start:stop, None]
        scores = jnp.where(allowed[None], scores, -1e30)
        peak = jnp.max(scores, axis=2, keepdims=True)
        weights = jnp.exp(scores - peak)
        total = jnp.sum(weights, axis=2, keepdims=True)
        mixed = jnp.einsum(
            "hqk,hkd->hqd",
            weights.astype(jnp.bfloat16),
            value_norm[:, :stop],
            preferred_element_type=jnp.float32,
        )
        pieces.append((mixed / total).astype(jnp.bfloat16))
    return jnp.concatenate(pieces, axis=1)


def fold_out(out_rows, gate, final_proj):
    top, low = split_two(out_rows.astype(jnp.float32) * gate[None, :])
    return dot32(final_proj, top, 1, 1) + dot32(final_proj, low, 1, 1)


def per_device(
    hidden_states,
    gen_weight,
    noise_field,
    timesteps,
    embed_real,
    time_real,
    query_real,
    key_real,
    value_real,
    out_real,
    gain_real,
    proj_real,
    embed_fake,
    time_fake,
    query_fake,
    key_fake,
    value_fake,
    out_fake,
    gain_fake,
    proj_fake,
):
    devices = lax.axis_size("tm")
    samples = lax.axis_size("batch")
    place = lax.axis_index("tm")
    frame_tokens = hidden_states.shape[1]
    tokens = frame_tokens * devices
    patch_rows = gen_weight.shape[0]
    width = gen_weight.shape[1]
    time_step = timesteps[0]
    level_raw = time_step.astype(jnp.float32) / 1000.0
    noise_level = 5.0 * level_raw / (1.0 + 4.0 * level_raw)
    generated = dot32(gen_weight, hidden_states[0], 1, 1).astype(jnp.bfloat16)
    noisy_patch = (
        (1.0 - noise_level) * generated.astype(jnp.float32)
        + noise_level * noise_field[0].astype(jnp.float32)
    ).astype(jnp.bfloat16)
    sinus_wave = sinusoid(time_step)
    freq_rows = time_real.shape[0]
    own_wave = lax.dynamic_slice_in_dim(sinus_wave, place * freq_rows, freq_rows, 0)
    shares = [
        jnp.einsum("f,fcd->cd", own_wave, table, preferred_element_type=jnp.float32)
        for table in (time_real, time_fake)
    ]
    shares = jnp.concatenate(shares).astype(jnp.bfloat16)
    modul_rows = shares.shape[0]
    payload = jnp.concatenate([noisy_patch, shares.reshape(-1, frame_tokens)])
    gathered = lax.all_gather(payload, "tm", axis=0, tiled=False)
    modul = jnp.sum(gathered[:, patch_rows:].astype(jnp.float32), axis=0)
    modul = modul.reshape(modul_rows, width)
    modul_real, modul_fake = modul[:3], modul[3:]
    patches = gathered[:, :patch_rows]
    patch_tokens = jnp.transpose(patches, (0, 2, 1)).reshape(tokens, patch_rows)
    prior = jnp.concatenate(
        [
            jnp.zeros((frame_tokens, patch_rows), jnp.bfloat16),
            patch_tokens[: tokens - frame_tokens],
        ]
    )
    token_rows = jnp.concatenate([patch_tokens, prior], axis=1)
    own_rows = lax.dynamic_slice_in_dim(token_rows, place * frame_tokens, frame_tokens, 0)

    def one_network(embed_table, modulation, query, key, value):
        centered = centre(embed_table)
        main, offset = fold_heads(centered, modulation[0], modulation[1], (query, key, value))
        return project(token_rows, gram_of(centered), main, offset)

    qkv_real = one_network(embed_real, modul_real, query_real, key_real, value_real)
    qkv_fake = one_network(embed_fake, modul_fake, query_fake, key_fake, value_fake)
    local_width = query_real.shape[1]
    columns = local_width * devices

    def columns_of(stacked, part):
        return stacked[:, part * local_width : (part + 1) * local_width]

    vectors = [
        columns_of(qkv_real, 0),
        columns_of(qkv_real, 1),
        columns_of(qkv_fake, 0),
        columns_of(qkv_fake, 1),
    ]
    squares = jnp.stack([jnp.sum(vector * vector, axis=1) for vector in vectors])
    norm_sums = jnp.sum(lax.all_gather(squares, "tm", axis=0, tiled=False), axis=0)
    gains = [gain_real[0], gain_real[1], gain_fake[0], gain_fake[1]]
    normed = [
        rms_round(vector, norm_sums[i], columns, gains[i]) for i, vector in enumerate(vectors)
    ]
    local_heads = local_width // HD

    def heads_of(parts):
        pieces = [
            part[:, h * HD : (h + 1) * HD] for part in parts for h in range(local_heads)
        ]
        return jnp.stack(pieces)

    attended = attend(
        heads_of((normed[0], normed[2])),
        heads_of((normed[1], normed[3])),
        heads_of(
            (
                columns_of(qkv_real, 2).astype(jnp.bfloat16),
                columns_of(qkv_fake, 2).astype(jnp.bfloat16),
            )
        ),
    )

    def head_terms(pieces, out_rows, gate, final_proj):
        flat = jnp.concatenate([pieces[h] for h in range(local_heads)], axis=1)
        framed = flat.reshape(devices, frame_tokens, local_width)
        top, low = split_two(fold_out(out_rows, gate, final_proj))
        terms = [
            jnp.einsum("pd,jtd->jpt", part, framed, preferred_element_type=jnp.float32)
            for part in (top, low)
        ]
        return terms[0] + terms[1]

    term_real = head_terms(attended[:local_heads], out_real, modul_real[2], proj_real)
    term_fake = head_terms(attended[local_heads:], out_fake, modul_fake[2], proj_fake)
    sent = jnp.concatenate([term_real, term_fake - term_real], axis=1).astype(jnp.bfloat16)
    landed = lax.all_to_all(sent, "tm", 0, 0, tiled=True)
    own_terms = jnp.sum(landed.astype(jnp.float32), axis=0)

    def base_of(final_proj, embed_table):
        top, low = split_two(dot32(final_proj, embed_table, 1, 1))
        return dot32(top, own_rows, 1, 1) + dot32(low, own_rows, 1, 1)

    base_real = base_of(proj_real, embed_real)
    base_fake = base_of(proj_fake, embed_fake)
    velocity_real = own_terms[:patch_rows] + base_real
    velocity_diff = own_terms[patch_rows:] + (base_fake - base_real)
    pred_real = noisy_patch.astype(jnp.float32) - noise_level * velocity_real
    gap_local = jnp.sum(jnp.abs(generated.astype(jnp.float32) - pred_real))
    gap_diff = -noise_level * velocity_diff
    difference = gap_diff.astype(jnp.bfloat16)
    partial_grad = jnp.dot(difference, hidden_states[0], preferred_element_type=jnp.float32)
    everyone = devices * samples
    lanes = 128
    blocks = jnp.transpose(
        partial_grad.astype(jnp.bfloat16).reshape(patch_rows, width // lanes, lanes), (1, 0, 2)
    ).reshape(everyone, -1, lanes)
    chunk_rows = blocks.shape[1]
    gap_top, gap_low = split_two(gap_local)
    lane = lax.broadcasted_iota(jnp.int32, (everyone, 16, lanes), 2)
    gap_rows = jnp.where(lane == 0, gap_top, gap_low)
    traded = lax.all_to_all(
        jnp.concatenate([blocks, gap_rows], axis=1), ("tm", "batch"), 0, 0, tiled=True
    ).astype(jnp.float32)
    gaps = traded[:, chunk_rows, 0] + traded[:, chunk_rows, 1]
    gap_total = jnp.sum(gaps.reshape(devices, samples), axis=0)
    count_all = patch_rows * tokens
    normalizers = jnp.maximum(gap_total / count_all, gap_floor)
    grad_root = math.sqrt(samples * hidden_states.shape[0] * tokens)
    per_source = jnp.tile(1.0 / (normalizers * grad_root), devices)
    own_chunk = jnp.sum(traded[:, :chunk_rows] * per_source[:, None, None], axis=0)
    whole = lax.all_gather(own_chunk.astype(jnp.bfloat16), ("tm", "batch"), axis=0, tiled=True)
    weight_grad = (
        jnp.transpose(whole.reshape(width // lanes, patch_rows, lanes), (1, 0, 2))
        .reshape(patch_rows, width)
        .astype(jnp.float32)
    )
    own_norm = lax.dynamic_index_in_dim(normalizers, lax.axis_index("batch"), 0, keepdims=False)
    dmd_gradient = (gap_diff / own_norm)[None]
    return (dmd_gradient, weight_grad)


def solution(mesh):
    in_specs = (
        P("batch", "tm", None),
        P(),
        P("batch", None, "tm"),
        P("batch"),
        P(),
        P("tm", None, None),
        P(None, "tm"),
        P(None, "tm"),
        P(None, "tm"),
        P("tm", None),
        P(None, "tm"),
        P(),
        P(),
        P("tm", None, None),
        P(None, "tm"),
        P(None, "tm"),
        P(None, "tm"),
        P("tm", None),
        P(None, "tm"),
        P(),
    )
    out_specs = (P("batch", None, "tm"), P())
    return jax.shard_map(
        per_device, mesh=mesh, in_specs=in_specs, out_specs=out_specs, check_vma=False
    )
```

```python
import math

import jax
import jax.numpy as jnp
from jax import lax
from jax.sharding import PartitionSpec as P

HD = 128
FREQ = 256
FTOK = 128


norm_floor = 0.05
gap_floor = 0.25


def sinusoid(time_step):
    half_freq = FREQ // 2
    frequency = jnp.exp(-math.log(10000.0) * jnp.arange(half_freq, dtype=jnp.float32) / half_freq)
    angles = time_step.astype(jnp.float32) * frequency
    return jnp.concatenate([jnp.cos(angles), jnp.sin(angles)]).astype(jnp.bfloat16)


def split_two(wide):
    top = lax.reduce_precision(wide, 8, 7)
    return top.astype(jnp.bfloat16), (wide - top).astype(jnp.bfloat16)


def dot32(left, right, left_dim, right_dim):
    return lax.dot_general(
        left, right, (((left_dim,), (right_dim,)), ((), ())), preferred_element_type=jnp.float32
    )


def centre(embed_table):
    wide = embed_table.astype(jnp.float32)
    return wide - jnp.mean(wide, axis=1, keepdims=True)


def gram_of(centered):
    top, low = split_two(centered)
    cross = dot32(top, low, 1, 1)
    return (dot32(top, top, 1, 1) + cross + cross.T) / centered.shape[1]


def fold_heads(centered, shift, scale, weights):
    rows = jnp.concatenate(
        [centered * (1.0 + scale)[None, :], jnp.broadcast_to(shift[None, :], (16, shift.shape[0]))]
    )
    count = rows.shape[0]
    both = jnp.concatenate(split_two(rows))
    folded = [dot32(both, weight, 1, 0) for weight in weights]
    folded = [piece[:count] + piece[count:] for piece in folded]
    kin_rows = centered.shape[0]
    main = jnp.concatenate([piece[:kin_rows] for piece in folded], axis=1)
    offset = jnp.concatenate([piece[kin_rows] for piece in folded])
    return main, offset


def project(token_rows, gram, main, offset):
    kin = token_rows.shape[1]
    table = jnp.concatenate(split_two(jnp.concatenate([main, gram], axis=1)))
    twice = jnp.concatenate([token_rows, token_rows], axis=1)
    product = dot32(twice, table, 1, 0)
    width = main.shape[1]
    variance = jnp.sum(product[:, width:] * token_rows.astype(jnp.float32), axis=1)
    rscale = lax.rsqrt(jnp.maximum(variance, 0.0) + norm_floor)
    return rscale[:, None] * product[:, :width] + offset[None, :]


def rms_round(vector, total_sq, columns, gain_row):
    return (
        vector * lax.rsqrt(total_sq / columns + norm_floor)[:, None] * gain_row[None, :]
    ).astype(jnp.bfloat16)


def attend(query_norm, key_norm, value_norm):
    tokens = query_norm.shape[1]
    block = min(256, tokens)
    frames = jnp.arange(tokens, dtype=jnp.int32) // FTOK
    pieces = []
    for start in range(0, tokens, block):
        stop = start + block
        scores = jnp.einsum(
            "hqd,hkd->hqk",
            query_norm[:, start:stop],
            key_norm[:, :stop],
            preferred_element_type=jnp.float32,
        ) / math.sqrt(HD)
        allowed = frames[None, :stop] <= frames[start:stop, None]
        scores = jnp.where(allowed[None], scores, -1e30)
        peak = jnp.max(scores, axis=2, keepdims=True)
        weights = jnp.exp(scores - peak)
        total = jnp.sum(weights, axis=2, keepdims=True)
        mixed = jnp.einsum(
            "hqk,hkd->hqd",
            weights.astype(jnp.bfloat16),
            value_norm[:, :stop],
            preferred_element_type=jnp.float32,
        )
        pieces.append((mixed / total).astype(jnp.bfloat16))
    return jnp.concatenate(pieces, axis=1)


def fold_out(out_rows, gate, final_proj):
    top, low = split_two(out_rows.astype(jnp.float32) * gate[None, :])
    return dot32(final_proj, top, 1, 1) + dot32(final_proj, low, 1, 1)


def per_device(
    hidden_states,
    gen_weight,
    noise_field,
    timesteps,
    embed_real,
    time_real,
    query_real,
    key_real,
    value_real,
    out_real,
    gain_real,
    proj_real,
    embed_fake,
    time_fake,
    query_fake,
    key_fake,
    value_fake,
    out_fake,
    gain_fake,
    proj_fake,
):
    devices = lax.axis_size("tm")
    samples = lax.axis_size("batch")
    place = lax.axis_index("tm")
    frame_tokens = hidden_states.shape[1]
    tokens = frame_tokens * devices
    patch_rows = gen_weight.shape[0]
    width = gen_weight.shape[1]
    time_step = timesteps[0]
    level_raw = time_step.astype(jnp.float32) / 1000.0
    noise_level = 5.0 * level_raw / (1.0 + 4.0 * level_raw)
    generated = dot32(gen_weight, hidden_states[0], 1, 1).astype(jnp.bfloat16)
    noisy_patch = (
        (1.0 - noise_level) * generated.astype(jnp.float32)
        + noise_level * noise_field[0].astype(jnp.float32)
    ).astype(jnp.bfloat16)
    sinus_wave = sinusoid(time_step)
    freq_rows = time_real.shape[0]
    own_wave = lax.dynamic_slice_in_dim(sinus_wave, place * freq_rows, freq_rows, 0)
    shares = [
        jnp.einsum("f,fcd->cd", own_wave, table, preferred_element_type=jnp.float32)
        for table in (time_real, time_fake)
    ]
    shares = jnp.concatenate(shares).astype(jnp.bfloat16)
    modul_rows = shares.shape[0]
    payload = jnp.concatenate([noisy_patch, shares.reshape(-1, frame_tokens)])
    gathered = lax.all_gather(payload, "tm", axis=0, tiled=False)
    modul = jnp.sum(gathered[:, patch_rows:].astype(jnp.float32), axis=0)
    modul = modul.reshape(modul_rows, width)
    modul_real, modul_fake = modul[:3], modul[3:]
    patches = gathered[:, :patch_rows]
    patch_tokens = jnp.transpose(patches, (0, 2, 1)).reshape(tokens, patch_rows)
    prior = jnp.concatenate(
        [
            jnp.zeros((frame_tokens, patch_rows), jnp.bfloat16),
            patch_tokens[: tokens - frame_tokens],
        ]
    )
    token_rows = jnp.concatenate([patch_tokens, prior], axis=1)
    own_rows = lax.dynamic_slice_in_dim(token_rows, place * frame_tokens, frame_tokens, 0)

    def one_network(embed_table, modulation, query, key, value):
        centered = centre(embed_table)
        main, offset = fold_heads(centered, modulation[0], modulation[1], (query, key, value))
        return project(token_rows, gram_of(centered), main, offset)

    qkv_real = one_network(embed_real, modul_real, query_real, key_real, value_real)
    qkv_fake = one_network(embed_fake, modul_fake, query_fake, key_fake, value_fake)
    local_width = query_real.shape[1]
    columns = local_width * devices

    def columns_of(stacked, part):
        return stacked[:, part * local_width : (part + 1) * local_width]

    vectors = [
        columns_of(qkv_real, 0),
        columns_of(qkv_real, 1),
        columns_of(qkv_fake, 0),
        columns_of(qkv_fake, 1),
    ]
    squares = jnp.stack([jnp.sum(vector * vector, axis=1) for vector in vectors])
    norm_sums = jnp.sum(lax.all_gather(squares, "tm", axis=0, tiled=False), axis=0)
    gains = [gain_real[0], gain_real[1], gain_fake[0], gain_fake[1]]
    normed = [
        rms_round(vector, norm_sums[i], columns, gains[i]) for i, vector in enumerate(vectors)
    ]
    local_heads = local_width // HD

    def heads_of(parts):
        pieces = [
            part[:, h * HD : (h + 1) * HD] for part in parts for h in range(local_heads)
        ]
        return jnp.stack(pieces)

    attended = attend(
        heads_of((normed[0], normed[2])),
        heads_of((normed[1], normed[3])),
        heads_of(
            (
                columns_of(qkv_real, 2).astype(jnp.bfloat16),
                columns_of(qkv_fake, 2).astype(jnp.bfloat16),
            )
        ),
    )

    def head_terms(pieces, out_rows, gate, final_proj):
        flat = jnp.concatenate([pieces[h] for h in range(local_heads)], axis=1)
        framed = flat.reshape(devices, frame_tokens, local_width)
        top, low = split_two(fold_out(out_rows, gate, final_proj))
        terms = [
            jnp.einsum("pd,jtd->jpt", part, framed, preferred_element_type=jnp.float32)
            for part in (top, low)
        ]
        return terms[0] + terms[1]

    term_real = head_terms(attended[:local_heads], out_real, modul_real[2], proj_real)
    term_fake = head_terms(attended[local_heads:], out_fake, modul_fake[2], proj_fake)
    sent = jnp.concatenate([term_real, term_fake - term_real], axis=1).astype(jnp.bfloat16)
    landed = lax.all_to_all(sent, "tm", 0, 0, tiled=True)
    own_terms = jnp.sum(landed.astype(jnp.float32), axis=0)

    def base_of(final_proj, embed_table):
        top, low = split_two(dot32(final_proj, embed_table, 1, 1))
        return dot32(top, own_rows, 1, 1) + dot32(low, own_rows, 1, 1)

    base_real = base_of(proj_real, embed_real)
    base_fake = base_of(proj_fake, embed_fake)
    velocity_real = own_terms[:patch_rows] + base_real
    velocity_diff = own_terms[patch_rows:] + (base_fake - base_real)
    pred_real = noisy_patch.astype(jnp.float32) - noise_level * velocity_real
    gap_local = jnp.sum(jnp.abs(generated.astype(jnp.float32) - pred_real))
    gap_diff = -noise_level * velocity_diff
    difference = gap_diff.astype(jnp.bfloat16)
    partial_grad = jnp.dot(difference, hidden_states[0], preferred_element_type=jnp.float32)
    lanes = 128
    blocks = jnp.transpose(
        partial_grad.astype(jnp.bfloat16).reshape(patch_rows, width // lanes, lanes), (1, 0, 2)
    ).reshape(devices, -1, lanes)
    chunk_rows = blocks.shape[1]
    gap_top, gap_low = split_two(gap_local)
    lane = lax.broadcasted_iota(jnp.int32, (devices, 16, lanes), 2)
    gap_rows = jnp.where(lane == 0, gap_top, gap_low)
    traded = lax.all_to_all(
        jnp.concatenate([blocks, gap_rows], axis=1), "tm", 0, 0, tiled=True
    ).astype(jnp.float32)
    gap_total = jnp.sum(traded[:, chunk_rows, 0] + traded[:, chunk_rows, 1])
    count_all = patch_rows * tokens
    own_norm = jnp.maximum(gap_total / count_all, gap_floor)
    grad_root = math.sqrt(samples * hidden_states.shape[0] * tokens)
    sample_chunk = jnp.sum(traded[:, :chunk_rows], axis=0) / own_norm / grad_root
    sample_chunks = lax.all_gather(sample_chunk.astype(jnp.bfloat16), "batch", axis=0, tiled=False)
    own_chunk = jnp.sum(sample_chunks.astype(jnp.float32), axis=0)
    whole = lax.all_gather(own_chunk.astype(jnp.bfloat16), "tm", axis=0, tiled=True)
    weight_grad = (
        jnp.transpose(whole.reshape(width // lanes, patch_rows, lanes), (1, 0, 2))
        .reshape(patch_rows, width)
        .astype(jnp.float32)
    )
    dmd_gradient = (gap_diff / own_norm)[None]
    return (dmd_gradient, weight_grad)


def solution(mesh):
    in_specs = (
        P("batch", "tm", None),
        P(),
        P("batch", None, "tm"),
        P("batch"),
        P(),
        P("tm", None, None),
        P(None, "tm"),
        P(None, "tm"),
        P(None, "tm"),
        P("tm", None),
        P(None, "tm"),
        P(),
        P(),
        P("tm", None, None),
        P(None, "tm"),
        P(None, "tm"),
        P(None, "tm"),
        P("tm", None),
        P(None, "tm"),
        P(),
    )
    out_specs = (P("batch", None, "tm"), P())
    return jax.shard_map(
        per_device, mesh=mesh, in_specs=in_specs, out_specs=out_specs, check_vma=False
    )
```
